32 devices in a mesh: parts: 2 (over x), tok: 16 (over z, y, core).
Axes of the slice: x: 2, y: 2, z: 4, core: 2. Of those that a mesh axis runs over, the one named last changes fastest.
Arguments:
- queries: bfloat16 [4096, 4096], P(('parts', 'tok')), parts along dimension 0, may hold values from -30 to 30
- keys: bfloat16 [4096, 512], P(('parts', 'tok')), parts along dimension 0, may hold values from -4 to 4
- values: bfloat16 [4096, 512], P(('parts', 'tok')), parts along dimension 0, may hold values from -5 to 5
- outputs: bfloat16 [4096, 4096], P(('parts', 'tok')), parts along dimension 0, may hold values from -3 to 3
- out_grad: bfloat16 [4096, 4096], P(('parts', 'tok')), parts along dimension 0, may hold values from -6 to 6
- ancestors: int32 [32, 10], P('parts'), parts along dimension 0, may hold values from -1 to 14, as said below
Outputs:
- query_grad: bfloat16 [4096, 4096], P(('parts', 'tok')), parts along dimension 0
- key_grad: bfloat16 [4096, 512], P(('parts', 'tok')), parts along dimension 0
- value_grad: bfloat16 [4096, 512], P(('parts', 'tok')), parts along dimension 0
The draws below stay inside these ranges and needn't reach their ends.
There are 2 independent parts, one for each index of `parts`. The reference program is written for one: setup_inputs(seed, part) draws one part's arguments, and reference() takes and returns one part's arrays. A program takes and returns all parts, laid end to end along the dimension named above; each array names one. Nothing has to cross between parts.
Inputs may be any that keep to these rules, and one draw needn't show every extreme that they name: Row t lists the ancestor tiles of tile t, from its parent up to tile 0, each once, then -1 to the end. Every listed tile is earlier than t; tile 0 is an ancestor of every other tile and has none; some tile has exactly 10 ancestors.
All inputs are finite; a program needn't handle non-finite values.
Results may differ from the reference program's by a relative error of at most 0.0053.
Values may be sent and summed in bfloat16 or wider, within the bound.
A program may use at most 128 MiB of HBM per device.

```python
import jax
import jax.numpy as jnp
from jax import lax

QH = 32
KVH = 4
HD = 128
TILE = 128
NT = 16
TOKENS = 2048
DEPTH = 10


def draw_queries(key, part):
    result = jnp.clip(jax.random.normal(jax.random.fold_in(key, 1), (TOKENS, QH, HD), jnp.float32), -4.0, 4.0)
    return result.reshape(TOKENS, QH * HD).astype(jnp.bfloat16)


def draw_keys(key, part):
    result = jnp.clip(jax.random.normal(jax.random.fold_in(key, 2), (TOKENS, KVH, HD), jnp.float32), -4.0, 4.0)
    return result.reshape(TOKENS, KVH * HD).astype(jnp.bfloat16)


def draw_ancestors(key, part):
    base_key = jax.random.fold_in(key, 23)
    chain_key, coin_key, pick_key = jax.random.split(base_key, 3)
    ranking = jnp.argsort(jax.random.randint(chain_key, (NT - 1,), 0, 1 << 30), stable=True).astype(jnp.int32) + 1
    chain = jnp.sort(ranking[:DEPTH]).astype(jnp.int32)
    in_chain = jnp.zeros((NT,), jnp.bool_).at[chain].set(True)
    chain_parent = jnp.zeros((NT,), jnp.int32).at[chain].set(jnp.concatenate([jnp.zeros((1,), jnp.int32), chain[:-1]]))
    coins = jax.random.randint(coin_key, (NT,), 0, 2)
    picks = jax.random.randint(pick_key, (NT,), 0, 1 << 30)

    def place(index, state):
        parents, depths = state
        guess = jnp.where(coins[index] == 1, index - 1, picks[index] % index).astype(jnp.int32)
        guess = jnp.where(depths[guess] >= DEPTH, parents[guess], guess)
        chosen_parent = jnp.where(in_chain[index], chain_parent[index], guess)
        return (parents.at[index].set(chosen_parent), depths.at[index].set(depths[chosen_parent] + 1))
    parents, depths = lax.fori_loop(1, NT, place, (jnp.full((NT,), -1, jnp.int32), jnp.zeros((NT,), jnp.int32)))
    columns = []
    current = parents
    for level in range(DEPTH):
        columns.append(current)
        current = jnp.where(current >= 0, parents[jnp.maximum(current, 0)], -1).astype(jnp.int32)
    return jnp.stack(columns, axis=1).astype(jnp.int32)


def levels(key, extent, cuts, low, largest):
    loudness, own = 1.0, jax.random.fold_in(key, 6)
    for dim, blocks in cuts:
        heights = jnp.exp(jax.random.uniform(jax.random.fold_in(own, dim), (blocks,), jnp.float32, low / len(cuts), largest / len(cuts)))
        loudness = loudness * jnp.repeat(heights, extent[dim] // blocks).reshape([-1 if axis == dim else 1 for axis in range(len(extent))])
    return loudness


def gaussian(stream_key, extent, spread, most, cuts=(), kind=jnp.bfloat16):
    values = spread * jax.random.normal(stream_key, extent, jnp.float32)
    if cuts:
        values = values * levels(stream_key, extent, cuts, -0.22, 0.18)
    return jnp.clip(values, -most, most).astype(kind)


def setup_inputs(seed: int = 0, part: int = 0) -> dict:
    key_of = jax.random.split(jax.random.key(seed), 7)
    part_splits = jax.random.split(jax.random.fold_in(key_of[6], part), 7)
    return {
        "queries": draw_queries(jax.random.fold_in(jax.random.fold_in(key_of[6], part), 71), part),
        "keys": draw_keys(jax.random.fold_in(jax.random.fold_in(key_of[6], part), 71), part),
        "values": gaussian(part_splits[2], (TOKENS, KVH * HD), 1.0, 5.0, ((0, 16),)),
        "outputs": gaussian(part_splits[3], (TOKENS, QH * HD), 0.5, 3.0, ((0, 16),)),
        "out_grad": gaussian(part_splits[4], (TOKENS, QH * HD), 1.0, 6.0, ((0, 16),)),
        "ancestors": draw_ancestors(jax.random.fold_in(jax.random.fold_in(key_of[6], part), 71), part),
    }


def reference(queries, keys, values, outputs, out_grad, ancestors):
    tile_count = ancestors.shape[0]
    slot_count = ancestors.shape[1] + 1
    groups = QH // KVH
    softmax_scale = HD ** -0.5
    query_tiles = queries.reshape(tile_count, TILE, KVH, groups, HD)
    output_tiles = outputs.reshape(tile_count, TILE, KVH, groups, HD)
    grad_tiles = out_grad.reshape(tile_count, TILE, KVH, groups, HD)
    key_tiles = keys.reshape(tile_count, TILE, KVH, HD)
    value_tiles = values.reshape(tile_count, TILE, KVH, HD)
    own_tiles = jnp.arange(tile_count, dtype=jnp.int32)[:, None]
    key_lists = jnp.concatenate([ancestors.astype(jnp.int32), own_tiles], axis=1)
    causal = jnp.arange(TILE)[:, None] >= jnp.arange(TILE)[None, :]
    not_self = jnp.arange(slot_count) != slot_count - 1

    def scan_step(carry, tile_index):
        key_acc, value_acc = carry
        tile_row = key_lists[tile_index]
        is_live = tile_row >= 0
        safe_tiles = jnp.maximum(tile_row, 0).astype(jnp.int32)
        key_block = key_tiles[safe_tiles].astype(jnp.float32)
        value_block = value_tiles[safe_tiles].astype(jnp.float32)
        query_block = query_tiles[tile_index].astype(jnp.float32)
        output_block = output_tiles[tile_index].astype(jnp.float32)
        grad_block = grad_tiles[tile_index].astype(jnp.float32)
        scores = jnp.einsum("ikgd,sjkd->kgisj", query_block, key_block) * softmax_scale
        key_mask = is_live[None, :, None] & (not_self[None, :, None] | causal[:, None, :])
        scores = jnp.where(key_mask, scores, -jnp.inf)
        row_max = jnp.max(scores, axis=(3, 4), keepdims=True)
        log_total = row_max + jnp.log(jnp.sum(jnp.exp(scores - row_max), axis=(3, 4), keepdims=True))
        attn_probs = jnp.exp(scores - log_total)
        probs_low = lax.optimization_barrier(attn_probs.astype(jnp.bfloat16)).astype(jnp.float32)
        grad_probs = jnp.einsum("ikgd,sjkd->kgisj", grad_block, value_block)
        row_delta = jnp.transpose(jnp.sum(grad_block * output_block, axis=-1), (1, 2, 0))[..., None, None]
        grad_scores = lax.optimization_barrier((attn_probs * (grad_probs - row_delta)).astype(jnp.bfloat16)).astype(jnp.float32)
        query_grad = (jnp.einsum("kgisj,sjkd->ikgd", grad_scores, key_block) * softmax_scale).astype(jnp.bfloat16)
        key_part = jnp.einsum("kgisj,ikgd->sjkd", grad_scores, query_block)
        value_part = jnp.einsum("kgisj,ikgd->sjkd", probs_low, grad_block)
        keep_mask = is_live[:, None, None, None]
        key_acc = key_acc.at[safe_tiles].add(jnp.where(keep_mask, key_part, 0.0))
        value_acc = value_acc.at[safe_tiles].add(jnp.where(keep_mask, value_part, 0.0))
        return (key_acc, value_acc), query_grad

    zeros_acc = jnp.zeros((tile_count, TILE, KVH, HD), jnp.float32)
    (key_acc, value_acc), query_grad = lax.scan(scan_step, (zeros_acc, zeros_acc), jnp.arange(tile_count, dtype=jnp.int32))
    token_count = tile_count * TILE
    key_grad = (key_acc * softmax_scale).astype(jnp.bfloat16).reshape(token_count, KVH * HD)
    value_grad = value_acc.astype(jnp.bfloat16).reshape(token_count, KVH * HD)
    return (query_grad.reshape(token_count, QH * HD), key_grad, value_grad)
```

```python
import functools
import math

import jax
import jax.numpy as jnp
from jax import lax
from jax.experimental import pallas as pl
from jax.experimental.pallas import tpu as pltpu
from jax.sharding import PartitionSpec as P

QH = 32
KVH = 4
HD = 128
TILE = 128
GROUP = QH // KVH
ROWS = GROUP * TILE
SCALE = HD ** -0.5
EXP_SCALE = SCALE * math.log2(math.e)
LOOP = lax.fori_loop
NY = 2
NC = 2


class Place:
    def __init__(self, tiles):
        self.nz = tiles // (NY * NC)
        tok = lax.axis_index("tok")
        self.me = tok
        self.z = tok // (NY * NC)
        self.y = lax.rem(tok // NC, NY)
        self.c = lax.rem(tok, NC)

    def at(self, z, y, c):
        return {"tok": (z * NY + y) * NC + c}

    def meet(self):
        barrier = pltpu.get_barrier_semaphore()

        def greet(d, carry):
            pl.semaphore_signal(
                barrier, 1, device_id=self.at(lax.rem(self.z + d, self.nz), self.y, self.c)
            )
            return carry

        LOOP(1, self.nz, greet, 0)
        pl.semaphore_signal(barrier, 1, device_id=self.at(self.z, 1 - self.y, self.c))
        pl.semaphore_signal(barrier, 1, device_id=self.at(self.z, self.y, 1 - self.c))
        pl.semaphore_wait(barrier, self.nz + 1)


def each(start, stop, body):
    def step(i, carry):
        body(i)
        return carry

    LOOP(start, stop, step, 0)


class Gather:
    def __init__(self, place, buf, sems):
        self.p, self.buf = place, buf
        self.zs, self.zr, self.ys, self.yr, self.cs, self.cr = sems

    @staticmethod
    def sems(nz):
        dma = pltpu.SemaphoreType.DMA
        return [
            dma((KVH, nz)), dma((KVH, nz)), dma((KVH, nz)), dma((KVH, nz)),
            dma((KVH, NY, nz)), dma((KVH, NY, nz)),
        ]

    def to_plane(self, g, src_z, dst_z):
        p = self.p
        block = self.buf.at[g, src_z, p.y, p.c]
        return pltpu.make_async_remote_copy(
            block, block, self.zs.at[g, dst_z], self.zr.at[g, src_z],
            device_id=p.at(dst_z, p.y, p.c))

    def to_y(self, g, z, y):
        p = self.p
        block = self.buf.at[g, z, y, p.c]
        return pltpu.make_async_remote_copy(
            block, block, self.ys.at[g, z], self.yr.at[g, z],
            device_id=p.at(p.z, 1 - p.y, p.c))

    def to_core(self, g, z, y, c):
        p = self.p
        block = self.buf.at[g, z, y, c]
        return pltpu.make_async_remote_copy(
            block, block, self.cs.at[g, y, z], self.cr.at[g, y, z],
            device_id=p.at(p.z, p.y, 1 - p.c))

    def first(self, g):
        p = self.p
        self.to_y(g, p.z, p.y).start()
        self.to_core(g, p.z, p.y, p.c).start()
        each(p.z + 1, p.nz, lambda dz: self.to_plane(g, p.z, dz).start())

    def second(self, g):
        p = self.p

        def step(z):
            self.to_plane(g, z, p.z).wait_recv()
            self.to_y(g, z, p.y).start()
            self.to_core(g, z, p.y, p.c).start()

        each(0, p.z, step)

    def third(self, g):
        p = self.p

        def step(z):
            self.to_y(g, z, 1 - p.y).wait_recv()
            self.to_core(g, z, 1 - p.y, p.c).start()

        each(0, p.z + 1, step)

    def fourth(self, g):
        p = self.p

        def step(z):
            self.to_core(g, z, 0, 1 - p.c).wait_recv()
            self.to_core(g, z, 1, 1 - p.c).wait_recv()

        each(0, p.z + 1, step)

    def drain(self, g):
        p = self.p
        each(p.z + 1, p.nz, lambda dz: self.to_plane(g, p.z, dz).wait_send())

        def step(z):
            self.to_y(g, z, p.y).wait_send()
            self.to_core(g, z, 0, p.c).wait_send()
            self.to_core(g, z, 1, p.c).wait_send()

        each(0, p.z + 1, step)


class Reduce:
    def __init__(self, place, part, scratch):
        self.p, self.part = place, part
        (self.from_core, self.for_y, self.from_y, self.for_z, self.from_z, self.own,
         self.cs, self.cr, self.ys, self.yr, self.zs, self.zr) = scratch

    @staticmethod
    def scratch(nz):
        dma = pltpu.SemaphoreType.DMA
        block = (2, TILE, HD)
        return [
            pltpu.VMEM((KVH, nz, NY) + block, jnp.bfloat16),
            pltpu.VMEM((KVH, nz) + block, jnp.bfloat16),
            pltpu.VMEM((KVH, nz) + block, jnp.bfloat16),
            pltpu.VMEM((KVH, nz) + block, jnp.bfloat16),
            pltpu.VMEM((KVH, nz) + block, jnp.bfloat16),
            pltpu.VMEM((KVH,) + block, jnp.float32),
        ] + [dma((KVH, NY, nz))] * 2 + [dma((KVH, nz))] * 4

    def to_core(self, g, z, y):
        p = self.p
        return pltpu.make_async_remote_copy(
            self.part.at[g, z, y, 1 - p.c], self.from_core.at[g, z, y],
            self.cs.at[g, y, z], self.cr.at[g, y, z],
            device_id=p.at(p.z, p.y, 1 - p.c))

    def to_y(self, g, z):
        p = self.p
        return pltpu.make_async_remote_copy(
            self.for_y.at[g, z], self.from_y.at[g, z], self.ys.at[g, z], self.yr.at[g, z],
            device_id=p.at(p.z, 1 - p.y, p.c))

    def to_plane(self, g, src_z, dst_z):
        p = self.p
        return pltpu.make_async_remote_copy(
            self.for_z.at[g, dst_z], self.from_z.at[g, src_z],
            self.zs.at[g, dst_z], self.zr.at[g, src_z],
            device_id=p.at(dst_z, p.y, p.c))

    def first(self, g):
        p = self.p

        def step(z):
            self.to_core(g, z, 1 - p.y).start()
            self.to_core(g, z, p.y).start()

        each(0, p.z + 1, step)

    def second(self, g):
        p = self.p

        def step(z):
            y = 1 - p.y
            self.to_core(g, z, y).wait_recv()
            total = self.part[g, z, y, p.c].astype(jnp.float32) + self.from_core[g, z, y].astype(jnp.float32)
            self.for_y[g, z] = total.astype(jnp.bfloat16)
            self.to_y(g, z).start()

        each(0, p.z + 1, step)

    def third(self, g):
        p = self.p

        def total(z):
            self.to_core(g, z, p.y).wait_recv()
            self.to_y(g, z).wait_recv()
            return (
                self.part[g, z, p.y, p.c].astype(jnp.float32)
                + self.from_core[g, z, p.y].astype(jnp.float32)
                + self.from_y[g, z].astype(jnp.float32)
            )

        def step(z):
            self.for_z[g, z] = total(z).astype(jnp.bfloat16)
            self.to_plane(g, p.z, z).start()

        each(0, p.z, step)
        self.own[g] = total(p.z)

    def fourth(self, g):
        p = self.p

        def step(z):
            self.to_plane(g, z, p.z).wait_recv()
            self.own[g] += self.from_z[g, z].astype(jnp.float32)

        each(p.z + 1, p.nz, step)

    def drain(self, g):
        p = self.p

        def step(z):
            self.to_core(g, z, 0).wait_send()
            self.to_core(g, z, 1).wait_send()
            self.to_y(g, z).wait_send()

        each(0, p.z + 1, step)
        each(0, p.z, lambda z: self.to_plane(g, p.z, z).wait_send())


def gather_kernel(tiles, k_ref, v_ref, buf, *sems):
    place = Place(tiles)
    gather = Gather(place, buf, sems)
    for g in range(KVH):
        columns = slice(g * HD, (g + 1) * HD)
        buf[g, place.z, place.y, place.c, 0] = k_ref[:, columns]
        buf[g, place.z, place.y, place.c, 1] = v_ref[:, columns]
    place.meet()
    heads = lambda step: each(0, KVH, step)
    heads(gather.first)
    heads(gather.second)
    heads(gather.third)
    heads(gather.fourth)
    heads(gather.drain)


def reduce_kernel(tiles, part, dk_ref, dv_ref, *scratch):
    place = Place(tiles)
    reduce = Reduce(place, part, scratch)
    place.meet()
    heads = lambda step: each(0, KVH, step)
    heads(reduce.first)
    heads(reduce.second)
    heads(reduce.third)
    heads(reduce.fourth)
    heads(reduce.drain)
    for g in range(KVH):
        columns = slice(g * HD, (g + 1) * HD)
        dk_ref[:, columns] = reduce.own[g, 0].astype(jnp.bfloat16)
        dv_ref[:, columns] = reduce.own[g, 1].astype(jnp.bfloat16)


def dot(a, b):
    return jnp.dot(a, b, preferred_element_type=jnp.float32)


def fold(x, op):
    return op(x.reshape(TILE // 8, 8, x.shape[-1]), axis=0)


def compute_kernel(
    table, q_ref, o_ref, g_ref, kv_ref, dq_ref, part_ref,
    qt, qs, gt, gs, delta, scores, peak, total, dqt,
):
    live = table[0]
    part_ref[...] = jnp.zeros_like(part_ref)
    for h in range(GROUP):
        columns = slice(h * TILE, (h + 1) * TILE)
        q, g = q_ref[:, columns], g_ref[:, columns]
        qs[columns, :] = q
        gs[columns, :] = g
        qt[:, columns] = q.T
        gt[:, columns] = g.T
        product = g.astype(jnp.float32) * o_ref[:, columns].astype(jnp.float32)
        delta[:, columns] = jnp.sum(product.T, axis=0, keepdims=True)

    own = table[1]
    s = dot(kv_ref[0, own, 0], qt[...])
    key_pos = lax.broadcasted_iota(jnp.int32, s.shape, 0)
    query_pos = lax.broadcasted_iota(jnp.int32, s.shape, 1) & (TILE - 1)
    s = jnp.where(key_pos <= query_pos, s, -1e30)
    scores[0] = s
    peak[...] = fold(s, jnp.max)

    def score(i):
        s = dot(kv_ref[0, table[1 + i], 0], qt[...])
        scores[i] = s
        peak[...] = jnp.maximum(peak[...], fold(s, jnp.max))

    each(1, live, score)
    top = jnp.max(peak[...], axis=0, keepdims=True)
    total[...] = jnp.zeros_like(total)

    def weigh(i):
        w = jnp.exp2((scores[i] - top) * EXP_SCALE)
        scores[i] = w
        total[...] += fold(w, jnp.sum)

    each(0, live, weigh)
    inverse = 1.0 / jnp.sum(total[...], axis=0, keepdims=True)
    dqt[...] = jnp.zeros_like(dqt)

    def back(i):
        tile = table[1 + i]
        k = kv_ref[0, tile, 0]
        p = scores[i] * inverse
        dp = dot(kv_ref[0, tile, 1], gt[...])
        ds = (p * (dp - delta[...])).astype(jnp.bfloat16)
        part_ref[0, tile, 1] = dot(p.astype(jnp.bfloat16), gs[...]).astype(jnp.bfloat16)
        part_ref[0, tile, 0] = (dot(ds, qs[...]) * SCALE).astype(jnp.bfloat16)
        dqt[...] += dot(k.T, ds)

    each(0, live, back)
    for h in range(GROUP):
        columns = slice(h * TILE, (h + 1) * TILE)
        dq_ref[:, columns] = (dqt[:, columns].T * SCALE).astype(jnp.bfloat16)


def per_device(tiles, queries, keys, values, outputs, out_grad, ancestors):
    depth = ancestors.shape[1]
    nz = tiles // (NY * NC)
    grid_shape = (KVH, nz, NY, NC, 2, TILE, HD)
    flat_shape = (KVH, tiles, 2, TILE, HD)
    vmem = pl.BlockSpec(memory_space=pltpu.VMEM)
    limit = 56 << 20
    gathered = pl.pallas_call(
        functools.partial(gather_kernel, tiles),
        out_shape=jax.ShapeDtypeStruct(grid_shape, jnp.bfloat16),
        in_specs=[vmem, vmem],
        out_specs=vmem,
        scratch_shapes=Gather.sems(nz),
        compiler_params=pltpu.CompilerParams(
            collective_id=0, has_side_effects=True, vmem_limit_bytes=limit),
    )(keys, values).reshape(flat_shape)

    me = lax.axis_index("tok").astype(jnp.int32)
    row = lax.dynamic_slice_in_dim(ancestors, me, 1, 0)[0]
    table = jnp.concatenate([(1 + jnp.sum((row >= 0).astype(jnp.int32)))[None], me[None], row])
    wide = pl.BlockSpec((TILE, ROWS), lambda g, t: (0, g))
    tall = pl.BlockSpec((1, tiles, 2, TILE, HD), lambda g, t: (g, 0, 0, 0, 0))
    f32, bf16 = jnp.float32, jnp.bfloat16
    query_grad, part = pl.pallas_call(
        compute_kernel,
        out_shape=(
            jax.ShapeDtypeStruct((TILE, QH * HD), bf16),
            jax.ShapeDtypeStruct(flat_shape, bf16),
        ),
        grid_spec=pltpu.PrefetchScalarGridSpec(
            num_scalar_prefetch=1,
            grid=(KVH,),
            in_specs=[wide, wide, wide, tall],
            out_specs=(wide, tall),
            scratch_shapes=[
                pltpu.VMEM((HD, ROWS), bf16),
                pltpu.VMEM((ROWS, HD), bf16),
                pltpu.VMEM((HD, ROWS), bf16),
                pltpu.VMEM((ROWS, HD), bf16),
                pltpu.VMEM((1, ROWS), f32),
                pltpu.VMEM((depth + 1, TILE, ROWS), f32),
                pltpu.VMEM((8, ROWS), f32),
                pltpu.VMEM((8, ROWS), f32),
                pltpu.VMEM((HD, ROWS), f32),
            ],
        ),
        compiler_params=pltpu.CompilerParams(vmem_limit_bytes=limit),
    )(table, queries, outputs, out_grad, gathered)

    key_grad, value_grad = pl.pallas_call(
        functools.partial(reduce_kernel, tiles),
        out_shape=(jax.ShapeDtypeStruct(keys.shape, bf16),) * 2,
        in_specs=[vmem],
        out_specs=(vmem, vmem),
        scratch_shapes=Reduce.scratch(nz),
        compiler_params=pltpu.CompilerParams(
            collective_id=1, has_side_effects=True, vmem_limit_bytes=limit),
    )(part.reshape(grid_shape))
    return query_grad, key_grad, value_grad


def solution(mesh):
    rows = P(("parts", "tok"), None)
    return jax.shard_map(
        functools.partial(per_device, mesh.shape["tok"]),
        mesh=mesh,
        in_specs=(rows,) * 5 + (P("parts", None),),
        out_specs=(rows,) * 3,
        check_vma=False,
    )
```

```python
import functools
import math

import jax
import jax.numpy as jnp
from jax import lax
from jax.experimental import pallas as pl
from jax.experimental.pallas import tpu as pltpu
from jax.sharding import PartitionSpec as P

QH = 32
KVH = 4
HD = 128
TILE = 128
GROUP = QH // KVH
ROWS = GROUP * TILE
SCALE = HD ** -0.5
EXP_SCALE = SCALE * math.log2(math.e)
LOOP = lax.fori_loop
NY = 2
NC = 2


class Place:
    def __init__(self, tiles):
        self.nz = tiles // (NY * NC)
        tok = lax.axis_index("tok")
        self.me = tok
        self.z = tok // (NY * NC)
        self.y = lax.rem(tok // NC, NY)
        self.c = lax.rem(tok, NC)

    def tile(self, z, y, c):
        return (z * NY + y) * NC + c

    def at(self, z, y, c):
        return {"tok": self.tile(z, y, c)}

    def meet(self):
        barrier = pltpu.get_barrier_semaphore()

        def greet(d, carry):
            pl.semaphore_signal(
                barrier, 1, device_id=self.at(lax.rem(self.z + d, self.nz), self.y, self.c)
            )
            return carry

        LOOP(1, self.nz, greet, 0)
        pl.semaphore_signal(barrier, 1, device_id=self.at(self.z, 1 - self.y, self.c))
        pl.semaphore_signal(barrier, 1, device_id=self.at(self.z, self.y, 1 - self.c))
        pl.semaphore_wait(barrier, self.nz + 1)


def each(start, stop, body):
    def step(i, carry):
        body(i)
        return carry

    LOOP(start, stop, step, 0)


class Gather:
    def __init__(self, place, buf, sems):
        self.p, self.buf = place, buf
        self.zs, self.zr, self.ys, self.yr, self.cs, self.cr = sems

    @staticmethod
    def sems(nz):
        dma = pltpu.SemaphoreType.DMA
        return [
            dma((KVH, nz)), dma((KVH, nz)), dma((KVH, nz)), dma((KVH, nz)),
            dma((KVH, NY, nz)), dma((KVH, NY, nz)),
        ]

    def to_plane(self, g, src_z, dst_z):
        p = self.p
        block = self.buf[g].at[p.tile(src_z, p.y, p.c)]
        return pltpu.make_async_remote_copy(
            block, block, self.zs.at[g, dst_z], self.zr.at[g, src_z],
            device_id=p.at(dst_z, p.y, p.c))

    def to_y(self, g, z, y):
        p = self.p
        block = self.buf[g].at[p.tile(z, y, p.c)]
        return pltpu.make_async_remote_copy(
            block, block, self.ys.at[g, z], self.yr.at[g, z],
            device_id=p.at(p.z, 1 - p.y, p.c))

    def to_core(self, g, z, y, c):
        p = self.p
        block = self.buf[g].at[p.tile(z, y, c)]
        return pltpu.make_async_remote_copy(
            block, block, self.cs.at[g, y, z], self.cr.at[g, y, z],
            device_id=p.at(p.z, p.y, 1 - p.c))

    def first(self, g):
        p = self.p
        self.to_y(g, p.z, p.y).start()
        self.to_core(g, p.z, p.y, p.c).start()
        each(p.z + 1, p.nz, lambda dz: self.to_plane(g, p.z, dz).start())

    def second(self, g):
        p = self.p

        def step(z):
            self.to_plane(g, z, p.z).wait_recv()
            self.to_y(g, z, p.y).start()
            self.to_core(g, z, p.y, p.c).start()

        each(0, p.z, step)

    def third(self, g):
        p = self.p

        def step(z):
            self.to_y(g, z, 1 - p.y).wait_recv()
            self.to_core(g, z, 1 - p.y, p.c).start()

        each(0, p.z + 1, step)

    def fourth(self, g):
        p = self.p

        def step(z):
            self.to_core(g, z, 0, 1 - p.c).wait_recv()
            self.to_core(g, z, 1, 1 - p.c).wait_recv()

        each(0, p.z + 1, step)

    def drain(self, g):
        p = self.p
        each(p.z + 1, p.nz, lambda dz: self.to_plane(g, p.z, dz).wait_send())

        def step(z):
            self.to_y(g, z, p.y).wait_send()
            self.to_core(g, z, 0, p.c).wait_send()
            self.to_core(g, z, 1, p.c).wait_send()

        each(0, p.z + 1, step)


class Reduce:
    def __init__(self, place, part, scratch):
        self.p, self.part = place, part
        (self.for_core, self.kept, self.from_core, self.for_y, self.from_y, self.for_z, self.from_z, self.own,
         self.cs, self.cr, self.ys, self.yr, self.zs, self.zr) = scratch

    @staticmethod
    def scratch(nz):
        dma = pltpu.SemaphoreType.DMA
        block = (2, TILE, HD)
        return [
            pltpu.VMEM((KVH, nz, NY) + block, jnp.bfloat16),
            pltpu.VMEM((KVH, nz, NY) + block, jnp.bfloat16),
            pltpu.VMEM((KVH, nz, NY) + block, jnp.bfloat16),
            pltpu.VMEM((KVH, nz) + block, jnp.bfloat16),
            pltpu.VMEM((KVH, nz) + block, jnp.bfloat16),
            pltpu.VMEM((KVH, nz) + block, jnp.bfloat16),
            pltpu.VMEM((KVH, nz) + block, jnp.bfloat16),
            pltpu.VMEM((KVH,) + block, jnp.float32),
        ] + [dma((KVH, NY, nz))] * 2 + [dma((KVH, nz))] * 4

    def to_core(self, g, z, y):
        p = self.p
        return pltpu.make_async_remote_copy(
            self.for_core.at[g, z, y], self.from_core.at[g, z, y],
            self.cs.at[g, y, z], self.cr.at[g, y, z],
            device_id=p.at(p.z, p.y, 1 - p.c))

    def to_y(self, g, z):
        p = self.p
        return pltpu.make_async_remote_copy(
            self.for_y.at[g, z], self.from_y.at[g, z], self.ys.at[g, z], self.yr.at[g, z],
            device_id=p.at(p.z, 1 - p.y, p.c))

    def to_plane(self, g, src_z, dst_z):
        p = self.p
        return pltpu.make_async_remote_copy(
            self.for_z.at[g, dst_z], self.from_z.at[g, src_z],
            self.zs.at[g, dst_z], self.zr.at[g, src_z],
            device_id=p.at(dst_z, p.y, p.c))

    def first(self, g, slot_of):
        p = self.p

        def block(z, y, c):
            slot = slot_of[p.tile(z, y, c)]
            values = self.part[jnp.maximum(slot, 0)]
            return jnp.where(slot >= 0, values, jnp.zeros_like(values))

        def step(z):
            for y in (1 - p.y, p.y):
                self.for_core[g, z, y] = block(z, y, 1 - p.c)
                self.to_core(g, z, y).start()
            for y in range(NY):
                self.kept[g, z, y] = block(z, y, p.c)

        each(0, p.z + 1, step)

    def second(self, g):
        p = self.p

        def step(z):
            y = 1 - p.y
            self.to_core(g, z, y).wait_recv()
            total = self.kept[g, z, y].astype(jnp.float32) + self.from_core[g, z, y].astype(jnp.float32)
            self.for_y[g, z] = total.astype(jnp.bfloat16)
            self.to_y(g, z).start()

        each(0, p.z + 1, step)

    def third(self, g):
        p = self.p

        def total(z):
            self.to_core(g, z, p.y).wait_recv()
            self.to_y(g, z).wait_recv()
            return (
                self.kept[g, z, p.y].astype(jnp.float32)
                + self.from_core[g, z, p.y].astype(jnp.float32)
                + self.from_y[g, z].astype(jnp.float32)
            )

        def step(z):
            self.for_z[g, z] = total(z).astype(jnp.bfloat16)
            self.to_plane(g, p.z, z).start()

        each(0, p.z, step)
        self.own[g] = total(p.z)

    def fourth(self, g):
        p = self.p

        def step(z):
            self.to_plane(g, z, p.z).wait_recv()
            self.own[g] += self.from_z[g, z].astype(jnp.float32)

        each(p.z + 1, p.nz, step)

    def drain(self, g):
        p = self.p

        def step(z):
            self.to_core(g, z, 0).wait_send()
            self.to_core(g, z, 1).wait_send()
            self.to_y(g, z).wait_send()

        each(0, p.z + 1, step)
        each(0, p.z, lambda z: self.to_plane(g, p.z, z).wait_send())


def dot(a, b):
    return jnp.dot(a, b, preferred_element_type=jnp.float32)


def fold(x, op):
    return op(x.reshape(TILE // 8, 8, x.shape[-1]), axis=0)


HALVES = (slice(0, TILE), slice(TILE, 2 * TILE))


def backward_kernel(
    tiles, pairs, table, slot_of, k_ref, v_ref, q_ref, o_ref, g_ref, dq_ref, dk_ref, dv_ref,
    qt, qs, gt, gs, delta, scores, slopes, peak, total, dqt, part, *rest,
):
    place = Place(tiles)
    buf, rest = rest[:KVH], rest[KVH:]
    gather = Gather(place, buf, rest[:6])
    reduce = Reduce(place, part, rest[6:])

    def head_columns(g):
        return slice(g * HD, (g + 1) * HD)

    for g in range(KVH):
        buf[g][place.me, 0] = k_ref[:, head_columns(g)]
        buf[g][place.me, 1] = v_ref[:, head_columns(g)]
    place.meet()

    def prepare(g):
        for h in range(GROUP):
            rows = slice(h * TILE, (h + 1) * TILE)
            columns = slice(g * ROWS + h * TILE, g * ROWS + (h + 1) * TILE)
            q, go = q_ref[:, columns], g_ref[:, columns]
            qs[rows, :] = q
            gs[rows, :] = go
            qt[:, rows] = q.T
            gt[:, rows] = go.T
            product = go.astype(jnp.float32) * o_ref[:, columns].astype(jnp.float32)
            delta[:, rows] = jnp.sum(product.T, axis=0, keepdims=True)
        s = dot(k_ref[:, head_columns(g)], qt[...])
        key_pos = lax.broadcasted_iota(jnp.int32, s.shape, 0)
        query_pos = lax.broadcasted_iota(jnp.int32, s.shape, 1) & (TILE - 1)
        s = jnp.where(key_pos <= query_pos, s, -1e30)
        scores[0] = s
        peak[...] = fold(s, jnp.max)
        slopes[0] = dot(v_ref[:, head_columns(g)], gt[...]) - delta[...]

    def tile_pair(g, i, which):
        return jnp.concatenate(
            [buf[g][jnp.maximum(table[2 * i + j], 0), which] for j in range(2)], axis=0
        )

    def score(g, i):
        s = dot(tile_pair(g, i, 0), qt[...])
        for j, half in enumerate(HALVES):
            scores[1 + 2 * i + j] = s[half]
            bias = jnp.where(table[2 * i + j] >= 0, 0.0, -1e30)
            peak[...] = jnp.maximum(peak[...], fold(s[half], jnp.max) + bias)

    def weigh_self(top):
        w = jnp.exp2((scores[0] - top) * EXP_SCALE)
        scores[0] = w
        total[...] = fold(w, jnp.sum)

    def weigh(g, i, top):
        slope = dot(tile_pair(g, i, 1), gt[...])
        for j, half in enumerate(HALVES):
            slot = 1 + 2 * i + j
            w = jnp.exp2((scores[slot] - top) * EXP_SCALE)
            w = jnp.where(table[2 * i + j] >= 0, w, 0.0)
            scores[slot] = w
            total[...] += fold(w, jnp.sum)
            slopes[slot] = slope[half] - delta[...]

    def back_self(g, inverse):
        p = scores[0] * inverse
        ds = (p * slopes[0]).astype(jnp.bfloat16)
        part[0, 1] = dot(p.astype(jnp.bfloat16), gs[...]).astype(jnp.bfloat16)
        part[0, 0] = (dot(ds, qs[...]) * SCALE).astype(jnp.bfloat16)
        dqt[...] = dot(k_ref[:, head_columns(g)].T, ds)

    def back(g, i, inverse):
        first = 1 + 2 * i
        p = scores[pl.ds(first, 2)].reshape(2 * TILE, ROWS) * inverse
        ds = (p * slopes[pl.ds(first, 2)].reshape(2 * TILE, ROWS)).astype(jnp.bfloat16)
        dv = dot(p.astype(jnp.bfloat16), gs[...]).astype(jnp.bfloat16)
        dk = (dot(ds, qs[...]) * SCALE).astype(jnp.bfloat16)
        for j, half in enumerate(HALVES):
            part[first + j, 0] = dk[half]
            part[first + j, 1] = dv[half]
        dqt[...] += dot(tile_pair(g, i, 0).T, ds)

    gather.first(0)
    gather.first(1)
    prepare(0)
    gather.second(0)
    gather.first(2)
    gather.third(0)
    gather.second(1)
    gather.first(3)
    for g in range(KVH):
        if g:
            prepare(g)
        gather.fourth(g)
        each(0, pairs, functools.partial(score, g))
        if g + 1 < KVH:
            gather.third(g + 1)
        if g:
            reduce.second(g - 1)
        top = jnp.max(peak[...], axis=0, keepdims=True)
        weigh_self(top)
        each(0, pairs, lambda i: weigh(g, i, top))
        if g + 2 < KVH:
            gather.second(g + 2)
        if g:
            reduce.third(g - 1)
        inverse = 1.0 / jnp.sum(total[...], axis=0, keepdims=True)
        back_self(g, inverse)
        each(0, pairs, lambda i: back(g, i, inverse))
        reduce.first(g, slot_of)
        for h in range(GROUP):
            rows = slice(h * TILE, (h + 1) * TILE)
            columns = slice(g * ROWS + h * TILE, g * ROWS + (h + 1) * TILE)
            dq_ref[:, columns] = (dqt[:, rows].T * SCALE).astype(jnp.bfloat16)
    reduce.second(KVH - 1)
    reduce.third(KVH - 1)
    for g in range(KVH):
        reduce.fourth(g)
        dk_ref[:, head_columns(g)] = reduce.own[g, 0].astype(jnp.bfloat16)
        dv_ref[:, head_columns(g)] = reduce.own[g, 1].astype(jnp.bfloat16)
    for g in range(KVH):
        gather.drain(g)
        reduce.drain(g)


def per_device(tiles, queries, keys, values, outputs, out_grad, ancestors):
    depth = ancestors.shape[1]
    pairs = (depth + 1) // 2
    slots = 1 + 2 * pairs
    nz = tiles // (NY * NC)
    me = lax.axis_index("tok").astype(jnp.int32)
    row = lax.dynamic_slice_in_dim(ancestors, me, 1, 0)[0]
    table = jnp.pad(row, (0, 2 * pairs - depth), constant_values=-1)
    listed = jnp.concatenate([me[None], table])
    match = listed[None, :] == jnp.arange(tiles, dtype=jnp.int32)[:, None]
    slot_of = jnp.max(jnp.where(match, jnp.arange(slots, dtype=jnp.int32)[None, :], -1), axis=1)
    vmem = pl.BlockSpec(memory_space=pltpu.VMEM)
    smem = pl.BlockSpec(memory_space=pltpu.SMEM)
    f32, bf16 = jnp.float32, jnp.bfloat16
    return pl.pallas_call(
        functools.partial(backward_kernel, tiles, pairs),
        out_shape=(
            jax.ShapeDtypeStruct(queries.shape, bf16),
            jax.ShapeDtypeStruct(keys.shape, bf16),
            jax.ShapeDtypeStruct(values.shape, bf16),
        ),
        in_specs=[smem] * 2 + [vmem] * 5,
        out_specs=(vmem,) * 3,
        scratch_shapes=[
            pltpu.VMEM((HD, ROWS), bf16),
            pltpu.VMEM((ROWS, HD), bf16),
            pltpu.VMEM((HD, ROWS), bf16),
            pltpu.VMEM((ROWS, HD), bf16),
            pltpu.VMEM((1, ROWS), f32),
            pltpu.VMEM((slots, TILE, ROWS), f32),
            pltpu.VMEM((slots, TILE, ROWS), f32),
            pltpu.VMEM((8, ROWS), f32),
            pltpu.VMEM((8, ROWS), f32),
            pltpu.VMEM((HD, ROWS), f32),
            pltpu.VMEM((slots, 2, TILE, HD), bf16),
        ]
        + [pltpu.VMEM((tiles, 2, TILE, HD), bf16)] * KVH
        + Gather.sems(nz)
        + Reduce.scratch(nz),
        compiler_params=pltpu.CompilerParams(
            collective_id=0, has_side_effects=True, vmem_limit_bytes=60 << 20),
    )(table, slot_of, keys, values, queries, outputs, out_grad)


def solution(mesh):
    rows = P(("parts", "tok"), None)
    return jax.shard_map(
        functools.partial(per_device, mesh.shape["tok"]),
        mesh=mesh,
        in_specs=(rows,) * 5 + (P("parts", None),),
        out_specs=(rows,) * 3,
        check_vma=False,
    )
```

```python
import functools
import math

import jax
import jax.numpy as jnp
from jax import lax
from jax.experimental import pallas as pl
from jax.experimental.pallas import tpu as pltpu
from jax.sharding import PartitionSpec as P

QH = 32
KVH = 4
HD = 128
TILE = 128
GROUP = QH // KVH
ROWS = GROUP * TILE
SCALE = HD ** -0.5
EXP_SCALE = SCALE * math.log2(math.e)
LOOP = lax.fori_loop
NY = 2
NC = 2


class Place:
    def __init__(self, tiles):
        self.nz = tiles // (NY * NC)
        tok = lax.axis_index("tok")
        self.me = tok
        self.z = tok // (NY * NC)
        self.y = lax.rem(tok // NC, NY)
        self.c = lax.rem(tok, NC)

    def tile(self, z, y, c):
        return (z * NY + y) * NC + c

    def at(self, z, y, c):
        return {"tok": self.tile(z, y, c)}

    def meet(self):
        barrier = pltpu.get_barrier_semaphore()

        def greet(d, carry):
            pl.semaphore_signal(
                barrier, 1, device_id=self.at(lax.rem(self.z + d, self.nz), self.y, self.c)
            )
            return carry

        LOOP(1, self.nz, greet, 0)
        pl.semaphore_signal(barrier, 1, device_id=self.at(self.z, 1 - self.y, self.c))
        pl.semaphore_signal(barrier, 1, device_id=self.at(self.z, self.y, 1 - self.c))
        pl.semaphore_wait(barrier, self.nz + 1)


def each(start, stop, body):
    def step(i, carry):
        body(i)
        return carry

    LOOP(start, stop, step, 0)


class Gather:
    def __init__(self, place, buf, sems):
        self.p, self.buf = place, buf
        self.zs, self.zr, self.ys, self.yr, self.cs, self.cr = sems

    @staticmethod
    def sems(nz):
        dma = pltpu.SemaphoreType.DMA
        return [
            dma((KVH, nz)), dma((KVH, nz)), dma((KVH, nz)), dma((KVH, nz)),
            dma((KVH, NY, nz)), dma((KVH, NY, nz)),
        ]

    def to_plane(self, g, src_z, dst_z):
        p = self.p
        block = self.buf[g].at[p.tile(src_z, p.y, p.c)]
        return pltpu.make_async_remote_copy(
            block, block, self.zs.at[g, dst_z], self.zr.at[g, src_z],
            device_id=p.at(dst_z, p.y, p.c))

    def to_y(self, g, z, y):
        p = self.p
        block = self.buf[g].at[p.tile(z, y, p.c)]
        return pltpu.make_async_remote_copy(
            block, block, self.ys.at[g, z], self.yr.at[g, z],
            device_id=p.at(p.z, 1 - p.y, p.c))

    def to_core(self, g, z, y, c):
        p = self.p
        block = self.buf[g].at[p.tile(z, y, c)]
        return pltpu.make_async_remote_copy(
            block, block, self.cs.at[g, y, z], self.cr.at[g, y, z],
            device_id=p.at(p.z, p.y, 1 - p.c))

    def first(self, g):
        p = self.p
        pl.when(p.y == 0)(lambda: self.to_y(g, p.z, p.y).start())
        self.to_core(g, p.z, p.y, p.c).start()
        each(p.z + 1, p.nz, lambda dz: self.to_plane(g, p.z, dz).start())

    def second(self, g):
        p = self.p

        def step(i):
            z = p.z - 1 - i
            self.to_plane(g, z, p.z).wait_recv()
            self.to_y(g, z, p.y).start()
            self.to_core(g, z, p.y, p.c).start()

        each(0, p.z, step)

    def third(self, g):
        p = self.p

        def step(i):
            z = p.z - i
            self.to_y(g, z, 1 - p.y).wait_recv()
            self.to_core(g, z, 1 - p.y, p.c).start()

        each(1 - p.y, p.z + 1, step)

    def fourth(self, g):
        p = self.p
        each(0, p.z + 1, lambda z: self.to_core(g, z, p.y, 1 - p.c).wait_recv())
        each(0, p.z + p.y, lambda z: self.to_core(g, z, 1 - p.y, 1 - p.c).wait_recv())

    def drain(self, g):
        p = self.p
        each(p.z + 1, p.nz, lambda dz: self.to_plane(g, p.z, dz).wait_send())
        each(0, p.z + 1 - p.y, lambda z: self.to_y(g, z, p.y).wait_send())
        each(0, p.z + 1, lambda z: self.to_core(g, z, p.y, p.c).wait_send())
        each(0, p.z + p.y, lambda z: self.to_core(g, z, 1 - p.y, p.c).wait_send())


class Reduce:
    def __init__(self, place, part, scratch):
        self.p, self.part = place, part
        (self.for_core, self.kept, self.from_core, self.for_y, self.from_y, self.for_z, self.from_z, self.own,
         self.cs, self.cr, self.ys, self.yr, self.zs, self.zr) = scratch

    @staticmethod
    def scratch(nz):
        dma = pltpu.SemaphoreType.DMA
        block = (2, TILE, HD)
        return [
            pltpu.VMEM((KVH, nz, NY) + block, jnp.bfloat16),
            pltpu.VMEM((KVH, nz, NY) + block, jnp.bfloat16),
            pltpu.VMEM((KVH, nz, NY) + block, jnp.bfloat16),
            pltpu.VMEM((KVH, nz) + block, jnp.bfloat16),
            pltpu.VMEM((KVH, nz) + block, jnp.bfloat16),
            pltpu.VMEM((KVH, nz) + block, jnp.bfloat16),
            pltpu.VMEM((KVH, nz) + block, jnp.bfloat16),
            pltpu.VMEM((KVH,) + block, jnp.float32),
        ] + [dma((KVH, NY, nz))] * 2 + [dma((KVH, nz))] * 4

    def to_core(self, g, z, y):
        p = self.p
        return pltpu.make_async_remote_copy(
            self.for_core.at[g, z, y], self.from_core.at[g, z, y],
            self.cs.at[g, y, z], self.cr.at[g, y, z],
            device_id=p.at(p.z, p.y, 1 - p.c))

    def to_y(self, g, z):
        p = self.p
        return pltpu.make_async_remote_copy(
            self.for_y.at[g, z], self.from_y.at[g, z], self.ys.at[g, z], self.yr.at[g, z],
            device_id=p.at(p.z, 1 - p.y, p.c))

    def to_plane(self, g, src_z, dst_z):
        p = self.p
        return pltpu.make_async_remote_copy(
            self.for_z.at[g, dst_z], self.from_z.at[g, src_z],
            self.zs.at[g, dst_z], self.zr.at[g, src_z],
            device_id=p.at(dst_z, p.y, p.c))

    def first(self, g, slot_of):
        p = self.p

        def block(z, y, c):
            slot = slot_of[p.tile(z, y, c)]
            values = self.part[jnp.maximum(slot, 0)]
            return jnp.where(slot >= 0, values, jnp.zeros_like(values))

        def give(y):
            def step(z):
                self.for_core[g, z, y] = block(z, y, 1 - p.c)
                self.to_core(g, z, y).start()

            return step

        def keep(z):
            for y in range(NY):
                self.kept[g, z, y] = block(z, y, p.c)

        each(0, p.z + p.y, give(1 - p.y))
        each(0, p.z + 1, give(p.y))
        each(0, p.z + 1, keep)

    def second(self, g):
        p = self.p

        def step(z):
            y = 1 - p.y
            self.to_core(g, z, y).wait_recv()
            total = self.kept[g, z, y].astype(jnp.float32) + self.from_core[g, z, y].astype(jnp.float32)
            self.for_y[g, z] = total.astype(jnp.bfloat16)
            self.to_y(g, z).start()

        each(0, p.z + p.y, step)

    def third(self, g):
        p = self.p

        def mine(z):
            self.to_core(g, z, p.y).wait_recv()
            return self.kept[g, z, p.y].astype(jnp.float32) + self.from_core[g, z, p.y].astype(jnp.float32)

        def across(z):
            self.to_y(g, z).wait_recv()
            return self.from_y[g, z].astype(jnp.float32)

        def step(z):
            self.for_z[g, z] = (mine(z) + across(z)).astype(jnp.bfloat16)
            self.to_plane(g, p.z, z).start()

        each(0, p.z, step)
        self.own[g] = mine(p.z)

        @pl.when(p.y == 0)
        def _():
            self.own[g] += across(p.z)

    def fourth(self, g):
        p = self.p

        def step(z):
            self.to_plane(g, z, p.z).wait_recv()
            self.own[g] += self.from_z[g, z].astype(jnp.float32)

        each(p.z + 1, p.nz, step)

    def drain(self, g):
        p = self.p
        each(0, p.z + 1, lambda z: self.to_core(g, z, p.y).wait_send())
        each(0, p.z + p.y, lambda z: self.to_core(g, z, 1 - p.y).wait_send())
        each(0, p.z + p.y, lambda z: self.to_y(g, z).wait_send())
        each(0, p.z, lambda z: self.to_plane(g, p.z, z).wait_send())


def dot(a, b):
    return jnp.dot(a, b, preferred_element_type=jnp.float32)


def dot_last(a, b):
    return lax.dot_general(
        a, b, (((1,), (1,)), ((), ())), preferred_element_type=jnp.float32)


def fold(x, op):
    return op(x.reshape(TILE // 8, 8, x.shape[-1]), axis=0)


HALVES = (slice(0, TILE), slice(TILE, 2 * TILE))


def backward_kernel(
    tiles, pairs, table, slot_of, k_ref, v_ref, q_ref, o_ref, g_ref, dq_ref, dk_ref, dv_ref,
    qs, gs, delta, scores, slopes, peak, total, dqt, part, *rest,
):
    place = Place(tiles)
    buf, rest = rest[:KVH], rest[KVH:]
    gather = Gather(place, buf, rest[:6])
    reduce = Reduce(place, part, rest[6:])

    def head_columns(g):
        return slice(g * HD, (g + 1) * HD)

    for g in range(KVH):
        buf[g][place.me, 0] = k_ref[:, head_columns(g)]
        buf[g][place.me, 1] = v_ref[:, head_columns(g)]
    place.meet()

    def stack(h, carry):
        rows = pl.ds(pl.multiple_of(h * TILE, TILE), TILE)
        q, go = q_ref[:, rows], g_ref[:, rows]
        qs[rows, :] = q
        gs[rows, :] = go
        product = go.astype(jnp.float32) * o_ref[:, rows].astype(jnp.float32)
        delta[:, rows] = jnp.sum(product.T, axis=0, keepdims=True)
        return carry

    def head_rows(g):
        return slice(g * ROWS, (g + 1) * ROWS)

    def self_score(g):
        s = dot_last(k_ref[:, head_columns(g)], qs[head_rows(g), :])
        key_pos = lax.broadcasted_iota(jnp.int32, s.shape, 0)
        query_pos = lax.broadcasted_iota(jnp.int32, s.shape, 1) & (TILE - 1)
        s = jnp.where(key_pos <= query_pos, s, -1e30)
        scores[0] = s
        peak[...] = fold(s, jnp.max)
        slopes[0] = dot_last(v_ref[:, head_columns(g)], gs[head_rows(g), :]) - delta[:, head_rows(g)]

    def tile_pair(g, i, which):
        return jnp.concatenate(
            [buf[g][jnp.maximum(table[2 * i + j], 0), which] for j in range(2)], axis=0
        )

    def score(g, i):
        s = dot_last(tile_pair(g, i, 0), qs[head_rows(g), :])
        for j, half in enumerate(HALVES):
            scores[1 + 2 * i + j] = s[half]
            bias = jnp.where(table[2 * i + j] >= 0, 0.0, -1e30)
            peak[...] = jnp.maximum(peak[...], fold(s[half], jnp.max) + bias)

    def weigh_self(top):
        w = jnp.exp2((scores[0] - top) * EXP_SCALE)
        scores[0] = w
        total[...] = fold(w, jnp.sum)

    def weigh(g, i, top):
        slope = dot_last(tile_pair(g, i, 1), gs[head_rows(g), :])
        for j, half in enumerate(HALVES):
            slot = 1 + 2 * i + j
            w = jnp.exp2((scores[slot] - top) * EXP_SCALE)
            w = jnp.where(table[2 * i + j] >= 0, w, 0.0)
            scores[slot] = w
            total[...] += fold(w, jnp.sum)
            slopes[slot] = slope[half] - delta[:, head_rows(g)]

    def back_self(g, inverse):
        p = scores[0] * inverse
        ds = (p * slopes[0]).astype(jnp.bfloat16)
        part[0, 1] = dot(p.astype(jnp.bfloat16), gs[head_rows(g), :]).astype(jnp.bfloat16)
        part[0, 0] = (dot(ds, qs[head_rows(g), :]) * SCALE).astype(jnp.bfloat16)
        dqt[...] = dot(k_ref[:, head_columns(g)].T, ds)

    def back(g, i, inverse):
        first = 1 + 2 * i
        p = scores[pl.ds(first, 2)].reshape(2 * TILE, ROWS) * inverse
        ds = (p * slopes[pl.ds(first, 2)].reshape(2 * TILE, ROWS)).astype(jnp.bfloat16)
        dv = dot(p.astype(jnp.bfloat16), gs[head_rows(g), :]).astype(jnp.bfloat16)
        dk = (dot(ds, qs[head_rows(g), :]) * SCALE).astype(jnp.bfloat16)
        for j, half in enumerate(HALVES):
            part[first + j, 0] = dk[half]
            part[first + j, 1] = dv[half]
        dqt[...] += dot(tile_pair(g, i, 0).T, ds)

    gather.first(0)
    LOOP(0, 2 * GROUP, stack, 0)
    gather.first(1)
    LOOP(2 * GROUP, KVH * GROUP, stack, 0)
    gather.first(2)
    self_score(0)
    gather.second(0)
    gather.first(3)
    gather.third(0)
    gather.second(1)
    for g in range(KVH):
        if g:
            self_score(g)
        gather.fourth(g)
        each(0, pairs, functools.partial(score, g))
        if g == 0:
            gather.second(2)
        if g + 1 < KVH:
            gather.third(g + 1)
        if g:
            reduce.second(g - 1)
        top = jnp.max(peak[...], axis=0, keepdims=True)
        weigh_self(top)
        each(0, pairs, lambda i: weigh(g, i, top))
        if g == 0:
            gather.second(3)
        inverse = 1.0 / jnp.sum(total[...], axis=0, keepdims=True)
        back_self(g, inverse)
        each(0, pairs, lambda i: back(g, i, inverse))
        reduce.first(g, slot_of)
        if g:
            reduce.third(g - 1)
        for h in range(GROUP):
            rows = slice(h * TILE, (h + 1) * TILE)
            columns = slice(g * ROWS + h * TILE, g * ROWS + (h + 1) * TILE)
            dq_ref[:, columns] = (dqt[:, rows].T * SCALE).astype(jnp.bfloat16)
    reduce.second(KVH - 1)
    reduce.third(KVH - 1)
    for g in range(KVH):
        reduce.fourth(g)
        dk_ref[:, head_columns(g)] = reduce.own[g, 0].astype(jnp.bfloat16)
        dv_ref[:, head_columns(g)] = reduce.own[g, 1].astype(jnp.bfloat16)
    for g in range(KVH):
        gather.drain(g)
        reduce.drain(g)


def per_device(tiles, queries, keys, values, outputs, out_grad, ancestors):
    depth = ancestors.shape[1]
    pairs = (depth + 1) // 2
    slots = 1 + 2 * pairs
    nz = tiles // (NY * NC)
    me = lax.axis_index("tok").astype(jnp.int32)
    row = lax.dynamic_slice_in_dim(ancestors, me, 1, 0)[0]
    table = jnp.pad(row, (0, 2 * pairs - depth), constant_values=-1)
    listed = jnp.concatenate([me[None], table])
    match = listed[None, :] == jnp.arange(tiles, dtype=jnp.int32)[:, None]
    slot_of = jnp.max(jnp.where(match, jnp.arange(slots, dtype=jnp.int32)[None, :], -1), axis=1)
    vmem = pl.BlockSpec(memory_space=pltpu.VMEM)
    smem = pl.BlockSpec(memory_space=pltpu.SMEM)
    f32, bf16 = jnp.float32, jnp.bfloat16
    return pl.pallas_call(
        functools.partial(backward_kernel, tiles, pairs),
        out_shape=(
            jax.ShapeDtypeStruct(queries.shape, bf16),
            jax.ShapeDtypeStruct(keys.shape, bf16),
            jax.ShapeDtypeStruct(values.shape, bf16),
        ),
        in_specs=[smem] * 2 + [vmem] * 5,
        out_specs=(vmem,) * 3,
        scratch_shapes=[
            pltpu.VMEM((KVH * ROWS, HD), bf16),
            pltpu.VMEM((KVH * ROWS, HD), bf16),
            pltpu.VMEM((1, KVH * ROWS), f32),
            pltpu.VMEM((slots, TILE, ROWS), f32),
            pltpu.VMEM((slots, TILE, ROWS), f32),
            pltpu.VMEM((8, ROWS), f32),
            pltpu.VMEM((8, ROWS), f32),
            pltpu.VMEM((HD, ROWS), f32),
            pltpu.VMEM((slots, 2, TILE, HD), bf16),
        ]
        + [pltpu.VMEM((tiles, 2, TILE, HD), bf16)] * KVH
        + Gather.sems(nz)
        + Reduce.scratch(nz),
        compiler_params=pltpu.CompilerParams(
            collective_id=0, has_side_effects=True, vmem_limit_bytes=60 << 20),
    )(table, slot_of, keys, values, queries, outputs, out_grad)


def solution(mesh):
    rows = P(("parts", "tok"), None)
    return jax.shard_map(
        functools.partial(per_device, mesh.shape["tok"]),
        mesh=mesh,
        in_specs=(rows,) * 5 + (P("parts", None),),
        out_specs=(rows,) * 3,
        check_vma=False,
    )
```
